128 devices in a mesh: row: 16 (over x, z), col: 8 (over y, core).
Axes of the slice: x: 4, y: 4, z: 4, core: 2. Of those that a mesh axis runs over, the one named last changes fastest.
Arguments:
- primal_rows: bfloat16 [16384, 8192], P('row', 'col'), may hold values from -6 to 6
- dual_rows: bfloat16 [16384, 8192], P('row', 'col'), may hold values from -6 to 6
- weight_rows: bfloat16 [16384, 8192], P('row', 'col'), may hold values from -0.0625 to 0.0625
- pairs: int32 [384, 2], P('row'), may hold values from 0 to 63, as said below
Outputs:
- tiles: float32 [384, 256, 256], P('row', 'col')
The draws below stay inside these ranges and needn't reach their ends.
Inputs may be any that keep to these rules, and one draw needn't show every extreme that they name: `pairs`: tile rows r * 24 to (r + 1) * 24 - 1 have their first block i among blocks r * 4 to (r + 1) * 4 - 1. Among their second blocks j, the blocks held by any other row index q (blocks q * 4 to (q + 1) * 4 - 1) are exactly one block, named one or more times; blocks of r itself may appear too.
All inputs are finite; a program needn't handle non-finite values.
Results may differ from the reference program's by a relative error of at most 0.0003.
Values may be sent and summed in bfloat16 or wider, within the bound.
No kernel may reach another device: no remote copies, remote signals or barrier semaphores. Data moves between devices by JAX's collectives and lax.ppermute only.
A program may use at most 128 MiB of HBM per device.

```python
import jax
import jax.numpy as jnp
from jax import lax

K = 8192
TILE = 256
BLK_DEV = 4
TCAP = 24
NEURONS = 16384
N_ROW = 16


def draw_pairs(key, part):
    subkeys = jax.random.split(jax.random.fold_in(key, 11), 4)
    owners = jnp.arange(N_ROW, dtype=jnp.int32)
    foreign = owners[None, :] * BLK_DEV + jax.random.randint(subkeys[0], (N_ROW, N_ROW), 0, BLK_DEV, dtype=jnp.int32)
    offsets = jnp.arange(N_ROW - 1, dtype=jnp.int32)
    sources = (owners[:, None] + 1 + offsets[None, :]) % N_ROW
    first_seconds = jnp.take_along_axis(foreign, sources, axis=1)
    local_all = owners[:, None] * BLK_DEV + jnp.arange(BLK_DEV, dtype=jnp.int32)[None, :]
    candidates = jnp.concatenate([local_all, first_seconds], axis=1)
    extra_count = TCAP - (N_ROW - 1)
    picked = jax.random.randint(subkeys[1], (N_ROW, extra_count), 0, BLK_DEV + N_ROW - 1, dtype=jnp.int32)
    extra_seconds = jnp.take_along_axis(candidates, picked, axis=1)
    seconds = jnp.concatenate([first_seconds, extra_seconds], axis=1)
    firsts = owners[:, None] * BLK_DEV + jax.random.randint(subkeys[2], (N_ROW, TCAP), 0, BLK_DEV, dtype=jnp.int32)
    scores = jax.random.randint(subkeys[3], (N_ROW, TCAP), 0, 1 << 20, dtype=jnp.int32) * TCAP + jnp.arange(TCAP, dtype=jnp.int32)[None, :]
    ranking = jnp.argsort(scores, axis=1, stable=True)
    seconds = jnp.take_along_axis(seconds, ranking, axis=1)
    return jnp.stack([firsts, seconds], axis=-1).reshape(N_ROW * TCAP, 2).astype(jnp.int32)


def level_of(own_key, shape, cuts, least, largest):
    gain = 1.0
    for dim, blocks in cuts:
        heights = jax.random.uniform(jax.random.fold_in(jax.random.fold_in(own_key, 6), dim), (blocks,), jnp.float32, least / len(cuts), largest / len(cuts))
        gain = gain * jnp.repeat(jnp.exp(heights), shape[dim] // blocks).reshape((-1,) + (1,) * (len(shape) - 1 - dim))
    return gain


def normal_values(rng, shape, deviation, bound, pieces=(), held_as=jnp.bfloat16):
    result = deviation * jax.random.normal(rng, shape, jnp.float32)
    if pieces:
        result = result * level_of(rng, shape, pieces, -0.22, 0.18)
    return jnp.clip(result, -bound, bound).astype(held_as)


def setup_inputs(seed: int = 0) -> dict:
    splits = jax.random.split(jax.random.key(seed), 5)
    return {
        "primal_rows": normal_values(splits[0], (NEURONS, K), 1.0, 6.0, ((0, 16), (1, 8))),
        "dual_rows": normal_values(splits[1], (NEURONS, K), 1.0, 6.0, ((0, 16), (1, 8))),
        "weight_rows": normal_values(splits[2], (NEURONS, K), K ** -0.5, 0.0625, ((0, 16), (1, 8))),
        "pairs": draw_pairs(jax.random.fold_in(splits[4], 71), 0),
    }


def reference(primal_rows, dual_rows, weight_rows, pairs):
    def one_tile(pair_row):
        first_start = (pair_row[0] * TILE).astype(jnp.int32)
        second_start = (pair_row[1] * TILE).astype(jnp.int32)
        left_x = lax.dynamic_slice_in_dim(primal_rows, first_start, TILE, 0).astype(jnp.float32)
        left_s = lax.dynamic_slice_in_dim(dual_rows, first_start, TILE, 0).astype(jnp.float32)
        right_rows = lax.dynamic_slice_in_dim(weight_rows, second_start, TILE, 0).astype(jnp.float32)
        cross_x = jnp.dot(left_x, right_rows.T, precision=lax.Precision.HIGHEST, preferred_element_type=jnp.float32)
        cross_s = jnp.dot(left_s, right_rows.T, precision=lax.Precision.HIGHEST, preferred_element_type=jnp.float32)
        return cross_x * cross_s

    return lax.map(one_tile, pairs)
```

```python
import functools

import jax
import jax.numpy as jnp
from jax import lax
from jax.experimental import pallas as pl
from jax.experimental.pallas import tpu as pltpu
from jax.sharding import PartitionSpec as P

TILE = 256
SIDE = 4
CHUNKS = 4

ANY = pl.BlockSpec(memory_space=pl.ANY)
SMEM = pl.BlockSpec(memory_space=pltpu.SMEM)


def shift_x(value, step):
    perm = [(r, ((r // SIDE + step) % SIDE) * SIDE + r % SIDE) for r in range(SIDE * SIDE)]
    return lax.ppermute(value, "row", perm)


def shift_z(value, step):
    perm = [(r, (r // SIDE) * SIDE + (r % SIDE + step) % SIDE) for r in range(SIDE * SIDE)]
    return lax.ppermute(value, "row", perm)


def shift_y(value, step):
    perm = [(c, ((c // 2 + step) % SIDE) * 2 + c % 2) for c in range(SIDE * 2)]
    return lax.ppermute(value, "col", perm)


def swap_cores(value):
    return lax.ppermute(value, "col", [(c, c ^ 1) for c in range(SIDE * 2)])


def pick_kernel(*refs):
    wants_z, wants_x = refs[0:4], refs[4:8]
    held = (refs[8:13], refs[13:18])
    outs = (refs[18:22], refs[22:26])
    sems = refs[26]
    row = lax.axis_index("row")
    x, z = row // SIDE, row % SIDE
    copies = []
    for half in range(2):
        own, plus, minus, far_low, far_high = held[half]
        for away in range(SIDE):
            for near in range(SIDE):
                if away == 0 and near == 0:
                    continue
                if half == 0:
                    source = ((x + SIDE - near) % SIDE) * SIDE + z
                    choice = wants_z[away][source]
                else:
                    source = x * SIDE + (z + SIDE - near) % SIDE
                    choice = wants_x[away][source]
                target = outs[half][away].at[near]
                sem = sems.at[half, away, near]
                if near == 2:
                    @pl.when(choice < 2)
                    def _():
                        pltpu.make_async_copy(far_low.at[choice], target, sem).start()

                    @pl.when(choice >= 2)
                    def _():
                        pltpu.make_async_copy(far_high.at[choice - 2], target, sem).start()
                else:
                    origin = {0: own, 1: plus, 3: minus}[near]
                    pltpu.make_async_copy(origin.at[choice], target, sem).start()
                copies.append((target, own.at[0], sem))
    for target, origin, sem in copies:
        pltpu.make_async_copy(origin, target, sem).wait()


def pick(wants_z, wants_x, held_a, held_b):
    part = held_a[0].shape[1:]
    piece = jax.ShapeDtypeStruct((SIDE,) + part, held_a[0].dtype)
    outs = pl.pallas_call(
        pick_kernel,
        out_shape=[piece] * 8,
        in_specs=[SMEM] * 8 + [ANY] * 10,
        out_specs=[ANY] * 8,
        scratch_shapes=[pltpu.SemaphoreType.DMA((2, SIDE, SIDE))],
    )(*wants_z, *wants_x, *held_a, *held_b)
    return outs[:4], outs[4:]


def product_kernel(per_step, *refs):
    pairs = refs[0]
    left_x, left_s = refs[1:3]
    tables = (refs[3:8], refs[8:13])
    mine, theirs = refs[13:15]
    held = refs[15:17]
    sems = refs[17]
    row, col = lax.axis_index("row"), lax.axis_index("col")
    x, z = row // SIDE, row % SIDE
    y, core = col // 2, col % 2
    step = pl.program_id(0)

    @pl.when(step == 0)
    def _():
        copies = []
        for half in range(2):
            for slot in range(5):
                copies.append(
                    pltpu.make_async_copy(
                        tables[half][slot],
                        held[half].at[pl.ds(slot * SIDE, SIDE)],
                        sems.at[half, slot],
                    )
                )
        for copy in copies:
            copy.start()
        for copy in copies:
            copy.wait()

    def one(n, carry):
        t = step * per_step + n
        first = pairs[2 * t] % 4
        second = pairs[2 * t + 1]
        q, block = second // 4, second % 4
        dx = (x + SIDE - q // SIDE) % SIDE
        dz = (z + SIDE - q % SIDE) % SIDE
        own = q == row
        slot_a = jnp.where(own, 16 + block, dz * SIDE + dx)
        slot_b = jnp.where(own, 16 + block, dx * SIDE + dz)
        right = jnp.concatenate([held[0][slot_a], held[1][slot_b]], axis=0)
        dims = (((1,), (1,)), ((), ()))
        out_x = lax.dot_general(left_x[first], right, dims, preferred_element_type=jnp.float32)
        out_s = lax.dot_general(left_s[first], right, dims, preferred_element_type=jnp.float32)
        both = jnp.concatenate([out_x, out_s], axis=1)
        parts = both.reshape(SIDE, 2, 32, both.shape[1])
        for target in range(SIDE):
            away = (target + SIDE - y) % SIDE
            for half in range(2):
                @pl.when(core == half)
                def _():
                    mine[away, n] = parts[target, half]

                @pl.when(core != half)
                def _():
                    theirs[away, n] = parts[target, half]
        return carry

    lax.fori_loop(0, per_step, one, 0)


def products(pairs, left_x, left_s, table_a, table_b, steps=4):
    tiles = pairs.shape[0] // 2
    rows = table_a[0].shape[1]
    features = left_x.shape[2]
    per_step = tiles // steps
    whole = pl.BlockSpec(left_x.shape, lambda s: (0, 0, 0), pipeline_mode=pl.Buffered(1))
    out_block = pl.BlockSpec((SIDE, per_step, 32, 4 * rows), lambda s: (0, s, 0, 0))
    piece = jax.ShapeDtypeStruct((SIDE, tiles, 32, 4 * rows), jnp.float32)
    return pl.pallas_call(
        functools.partial(product_kernel, per_step),
        grid=(steps,),
        out_shape=[piece, piece],
        in_specs=[SMEM, whole, whole] + [ANY] * 10,
        out_specs=[out_block, out_block],
        scratch_shapes=[
            pltpu.VMEM((20, rows, features), jnp.bfloat16),
            pltpu.VMEM((20, rows, features), jnp.bfloat16),
            pltpu.SemaphoreType.DMA((2, 5)),
        ],
    )(pairs, left_x, left_s, *table_a, *table_b)


def gather_ring(own, shift):
    plus = shift(own, 1)
    minus = shift(own, SIDE - 1)
    far_low = shift(plus[:2], 1)
    far_high = shift(minus[2:], SIDE - 1)
    return own, plus, minus, far_low, far_high


def shards(primal_rows, dual_rows, weight_rows, pairs):
    features = primal_rows.shape[1]
    blocks = primal_rows.shape[0] // TILE
    weight = weight_rows.reshape(blocks, TILE, features)
    left_x = primal_rows.reshape(blocks, TILE, features)
    left_s = dual_rows.reshape(blocks, TILE, features)
    flat_pairs = pairs.reshape(-1)
    second = pairs[:, 1]
    hit = second[:, None] // blocks == jnp.arange(SIDE * SIDE, dtype=jnp.int32)[None, :]
    want = jnp.max(jnp.where(hit, second[:, None] % blocks, 0), axis=0)
    wants_z = [want] + [shift_z(want, SIDE - d) for d in range(1, SIDE)]
    wants_x = [want] + [shift_x(want, SIDE - d) for d in range(1, SIDE)]
    width = TILE // CHUNKS
    half = width // 2
    outs = []
    for chunk in range(CHUNKS):
        start = chunk * width
        held_a = gather_ring(weight[:, start : start + half], shift_x)
        held_b = gather_ring(weight[:, start + half : start + width], shift_z)
        send_a, send_b = pick(wants_z, wants_x, held_a, held_b)
        table_a = [send_a[0]] + [shift_z(send_a[d], d) for d in range(1, SIDE)] + [held_a[0]]
        table_b = [send_b[0]] + [shift_x(send_b[d], d) for d in range(1, SIDE)] + [held_b[0]]
        mine, theirs = products(flat_pairs, left_x, left_s, table_a, table_b)
        total = mine + swap_cores(theirs)
        summed = total[0]
        for d in range(1, SIDE):
            summed = summed + shift_y(total[d], d)
        outs.append(summed[..., :width] * summed[..., width:])
    return jnp.concatenate(outs, axis=-1)


def solution(mesh):
    placed = (P("row", "col"), P("row", "col"), P("row", "col"), P("row", None))
    return jax.shard_map(
        shards, mesh=mesh, in_specs=placed, out_specs=P("row", "col", None), check_vma=False
    )
```

```python
import functools

import jax
import jax.numpy as jnp
from jax import lax
from jax.experimental import pallas as pl
from jax.experimental.pallas import tpu as pltpu
from jax.sharding import PartitionSpec as P

TILE = 256
SIDE = 4
WIDTHS = (128, 128)
LANES = 128
ROWS = 32
TOP = 32700.0

ANY = pl.BlockSpec(memory_space=pl.ANY)
SMEM = pl.BlockSpec(memory_space=pltpu.SMEM)
VMEM = pl.BlockSpec(memory_space=pltpu.VMEM)


def shift_x(value, step):
    perm = [(r, ((r // SIDE + step) % SIDE) * SIDE + r % SIDE) for r in range(SIDE * SIDE)]
    return lax.ppermute(value, "row", perm)


def shift_z(value, step):
    perm = [(r, (r // SIDE) * SIDE + (r % SIDE + step) % SIDE) for r in range(SIDE * SIDE)]
    return lax.ppermute(value, "row", perm)


def shift_y(value, step):
    perm = [(c, ((c // 2 + step) % SIDE) * 2 + c % 2) for c in range(SIDE * 2)]
    return lax.ppermute(value, "col", perm)


def swap_cores(value):
    return lax.ppermute(value, "col", [(c, c ^ 1) for c in range(SIDE * 2)])


def pick_kernel(offset, *refs):
    wants_z, wants_x = refs[0:4], refs[4:8]
    held = (refs[8:13], refs[13:18])
    outs = (refs[18:22], refs[22:26])
    sems = refs[26]
    part = pl.ds(offset, outs[0][0].shape[1])
    row = lax.axis_index("row")
    x, z = row // SIDE, row % SIDE
    waits = []
    for half in range(2):
        own, plus, minus, far_low, far_high = held[half]
        for away in range(SIDE):
            for near in range(SIDE):
                if away == 0 and near == 0:
                    continue
                if half == 0:
                    choice = wants_z[away][((x + SIDE - near) % SIDE) * SIDE + z]
                else:
                    choice = wants_x[away][x * SIDE + (z + SIDE - near) % SIDE]
                target = outs[half][away].at[near]
                sem = sems.at[half, away, near]
                if near == 2:
                    @pl.when(choice < 2)
                    def _():
                        pltpu.make_async_copy(far_low.at[choice, part], target, sem).start()

                    @pl.when(choice >= 2)
                    def _():
                        pltpu.make_async_copy(far_high.at[choice - 2, part], target, sem).start()
                else:
                    origin = {0: own, 1: plus, 3: minus}[near]
                    pltpu.make_async_copy(origin.at[choice, part], target, sem).start()
                waits.append(pltpu.make_async_copy(own.at[0, part], target, sem))
    for copy in waits:
        copy.wait()


def pick(wants_z, wants_x, held_a, held_b, offset, rows):
    piece = jax.ShapeDtypeStruct((SIDE, rows, held_a[0].shape[2]), held_a[0].dtype)
    outs = pl.pallas_call(
        functools.partial(pick_kernel, offset),
        out_shape=[piece] * 8,
        in_specs=[SMEM] * 8 + [ANY] * 10,
        out_specs=[VMEM] * 8,
        scratch_shapes=[pltpu.SemaphoreType.DMA((2, SIDE, SIDE))],
        name=f"pick_{offset}",
    )(*wants_z, *wants_x, *held_a, *held_b)
    return outs[:4], outs[4:]


def product_kernel(offset, rows, slots, *refs):
    group_first, slot_tile, slot_a, slot_b, left_x, left_s = refs[0:6]
    tables = (refs[6:11], refs[11:16])
    mine, theirs = refs[16:18]
    left, held_a, held_b, acc, sems, out_sems = refs[18:]
    col = lax.axis_index("col")
    y, core = col // 2, col % 2
    width = 2 * rows
    group = TILE // width
    blocks = mine.shape[1]
    copies = [
        pltpu.make_async_copy(left_x, left.at[:, pl.ds(0, TILE)], sems.at[2, 0]),
        pltpu.make_async_copy(left_s, left.at[:, pl.ds(TILE, TILE)], sems.at[2, 1]),
    ]
    for half, held in enumerate((held_a, held_b)):
        for place in range(5):
            source = tables[half][place]
            if place == 4:
                source = source.at[:, pl.ds(offset, rows)]
            copies.append(
                pltpu.make_async_copy(source, held.at[pl.ds(place * SIDE, SIDE)], sems.at[half, place])
            )
    for copy in copies:
        copy.start()
    for copy in copies:
        copy.wait()

    def one(slot, carry):
        right = []
        for g in range(group):
            right += [held_a[slot_a[slot * group + g]], held_b[slot_b[slot * group + g]]]
        out = lax.dot_general(
            left[group_first[slot]],
            jnp.concatenate(right, axis=0),
            (((1,), (1,)), ((), ())),
            preferred_element_type=jnp.float32,
        )
        for g in range(group):
            tile = slot_tile[slot * group + g]
            cross_x = out[:TILE, g * width : (g + 1) * width]
            cross_s = out[TILE:, g * width : (g + 1) * width]
            if width == LANES:
                pieces = (cross_x, cross_s)
            else:
                pieces = (jnp.concatenate([cross_x, cross_s], axis=1),)
            for n, piece in enumerate(pieces):
                parts = piece.reshape(SIDE, 2, ROWS, LANES)
                for target in range(SIDE):
                    away = (target + SIDE - y) % SIDE
                    for half in range(2):
                        acc[jnp.bitwise_xor(core, half), away, tile * len(pieces) + n] = parts[target, half]
        return carry

    lax.fori_loop(0, slots, one, 0, unroll=2 if slots % 2 == 0 else 3)
    out_copies = [
        pltpu.make_async_copy(acc.at[1, :, pl.ds(0, blocks)], theirs, out_sems.at[1]),
        pltpu.make_async_copy(acc.at[0, :, pl.ds(0, blocks)], mine, out_sems.at[0]),
    ]
    for copy in out_copies:
        copy.start()
    for copy in out_copies:
        copy.wait()


def grouped(first, spot_a, spot_b, group):
    tiles = first.shape[0]
    slots = (tiles + (group - 1) * SIDE) // group
    kinds = jnp.arange(SIDE, dtype=jnp.int32)
    order = jnp.arange(tiles, dtype=jnp.int32)
    same = first[:, None] == first[None, :]
    rank = jnp.sum(jnp.where(same & (order[None, :] < order[:, None]), 1, 0), axis=1)
    counts = jnp.sum(jnp.where(first[None, :] == kinds[:, None], 1, 0), axis=1)
    sizes = (counts + group - 1) // group
    starts = jnp.sum(jnp.where(kinds[None, :] < kinds[:, None], sizes[None, :], 0), axis=1)
    start = jnp.sum(jnp.where(first[:, None] == kinds[None, :], starts[None, :], 0), axis=1)
    place = start * group + rank
    chosen = place[None, :] == jnp.arange(slots * group, dtype=jnp.int32)[:, None]
    used = jnp.any(chosen, axis=1)
    pull = lambda v: jnp.sum(jnp.where(chosen, v[None, :], 0), axis=1)
    slot_tile = jnp.where(used, pull(order), tiles)
    slot_a = jnp.where(used, pull(spot_a), 16)
    slot_b = jnp.where(used, pull(spot_b), 16)
    past = jnp.arange(slots, dtype=jnp.int32)[:, None] >= starts[None, :]
    group_first = jnp.sum(jnp.where(past, 1, 0), axis=1) - 1
    return slots, (group_first, slot_tile, slot_a, slot_b)


def products(lists, slots, left_x, left_s, table_a, table_b, offset, rows, tiles):
    features = left_x.shape[2]
    per_tile = 2 * rows // 64
    piece = jax.ShapeDtypeStruct((SIDE, tiles * per_tile, ROWS, LANES), jnp.float32)
    return pl.pallas_call(
        functools.partial(product_kernel, offset, rows, slots),
        out_shape=[piece, piece],
        in_specs=[SMEM] * 4 + [ANY] * 12,
        out_specs=[ANY, ANY],
        scratch_shapes=[
            pltpu.VMEM((SIDE, 2 * TILE, features), jnp.bfloat16),
            pltpu.VMEM((20, rows, features), jnp.bfloat16),
            pltpu.VMEM((20, rows, features), jnp.bfloat16),
            pltpu.VMEM((2, SIDE, (tiles + 1) * per_tile, ROWS, LANES), jnp.float32),
            pltpu.SemaphoreType.DMA((3, 5)),
            pltpu.SemaphoreType.DMA((2,)),
        ],
        name=f"products_{offset}",
    )(*lists, left_x, left_s, *table_a, *table_b)


def merge_kernel(mine, theirs, kept, *coded):
    count = kept.shape[0]
    kept[...] = mine[0] + theirs[0]
    for d in range(1, SIDE):
        value = mine[d] + theirs[d]
        peak = jnp.maximum(jnp.max(jnp.abs(value), axis=1), 1e-30)
        level = jnp.ceil(jnp.log2(peak) * 256.0)
        factor = jnp.exp2(level * (-1.0 / 256.0)) * TOP
        code = jnp.round(value * factor[:, None, :]).astype(jnp.int32).astype(jnp.int16)
        out = coded[d - 1]
        out[pl.ds(0, count * ROWS)] = code.reshape(count * ROWS, LANES)
        levels = level.astype(jnp.int32)
        spare = out.shape[0] - count * ROWS - count
        if spare:
            levels = jnp.concatenate([levels, jnp.zeros((spare, LANES), jnp.int32)], axis=0)
        out[pl.ds(count * ROWS, count + spare)] = levels.astype(jnp.int16)


def step_sizes(blocks):
    count = 16 if blocks % 16 == 0 else blocks
    return count, blocks // count, count * ROWS + -(-count // 16) * 16


def merge(mine, theirs):
    blocks = mine.shape[1]
    count, steps, length = step_sizes(blocks)
    wide = pl.BlockSpec((SIDE, count, ROWS, LANES), lambda s: (0, s, 0, 0))
    return pl.pallas_call(
        merge_kernel,
        grid=(steps,),
        out_shape=[jax.ShapeDtypeStruct((blocks, ROWS, LANES), jnp.float32)]
        + [jax.ShapeDtypeStruct((steps * length, LANES), jnp.int16)] * 3,
        in_specs=[wide, wide],
        out_specs=[pl.BlockSpec((count, ROWS, LANES), lambda s: (s, 0, 0))]
        + [pl.BlockSpec((length, LANES), lambda s: (s, 0))] * 3,
        name="merge",
    )(mine, theirs)


def finish_kernel(per_tile, kept, *refs):
    coded, out = refs[:3], refs[3]
    count = kept.shape[0]
    total = kept[...]
    for ref in coded:
        code = ref[pl.ds(0, count * ROWS)].astype(jnp.int32).astype(jnp.float32)
        levels = ref[pl.ds(count * ROWS, ref.shape[0] - count * ROWS)]
        levels = levels.astype(jnp.int32).astype(jnp.float32)[:count]
        factor = jnp.exp2(levels * (1.0 / 256.0)) * (1.0 / TOP)
        total = total + code.reshape(count, ROWS, LANES) * factor[:, None, :]
    if per_tile == 2:
        pairs = total.reshape(count // 2, 2, ROWS, LANES)
        out[...] = pairs[:, 0] * pairs[:, 1]
    else:
        out[...] = total[..., : LANES // 2] * total[..., LANES // 2 :]


def finish(kept, coded, per_tile):
    blocks = kept.shape[0]
    count, steps, length = step_sizes(blocks)
    tiles = count // per_tile
    width = 64 * per_tile
    return pl.pallas_call(
        functools.partial(finish_kernel, per_tile),
        grid=(steps,),
        out_shape=jax.ShapeDtypeStruct((tiles * steps, ROWS, width), jnp.float32),
        in_specs=[pl.BlockSpec((count, ROWS, LANES), lambda s: (s, 0, 0))]
        + [pl.BlockSpec((length, LANES), lambda s: (s, 0))] * 3,
        out_specs=pl.BlockSpec((tiles, ROWS, width), lambda s: (s, 0, 0)),
        name="finish",
    )(kept, *coded)


def gather_ring(own, shift):
    plus = shift(own, 1)
    minus = shift(own, SIDE - 1)
    far_low = shift(plus[:2], 1)
    far_high = shift(minus[2:], SIDE - 1)
    return own, plus, minus, far_low, far_high


def shards(primal_rows, dual_rows, weight_rows, pairs):
    row = lax.axis_index("row")
    x, z = row // SIDE, row % SIDE
    features = primal_rows.shape[1]
    blocks = primal_rows.shape[0] // TILE
    tiles = pairs.shape[0]
    weight = weight_rows.reshape(blocks, TILE, features)
    left_x = primal_rows.reshape(blocks, TILE, features)
    left_s = dual_rows.reshape(blocks, TILE, features)

    starts = [sum(WIDTHS[:k]) for k in range(len(WIDTHS))]
    half_a = [weight[:, s : s + w // 2] for s, w in zip(starts, WIDTHS)]
    half_b = [weight[:, s + w // 2 : s + w] for s, w in zip(starts, WIDTHS)]
    held_a = gather_ring(jnp.concatenate(half_a, axis=1), shift_x)
    held_b = gather_ring(jnp.concatenate(half_b, axis=1), shift_z)

    second = pairs[:, 1]
    owner, local = second // blocks, second % blocks
    hit = owner[:, None] == jnp.arange(SIDE * SIDE, dtype=jnp.int32)[None, :]
    want = jnp.max(jnp.where(hit, local[:, None], 0), axis=0)
    wants_z = [want] + [shift_z(want, SIDE - d) for d in range(1, SIDE)]
    wants_x = [want] + [shift_x(want, SIDE - d) for d in range(1, SIDE)]
    dx = (x + SIDE - owner // SIDE) % SIDE
    dz = (z + SIDE - owner % SIDE) % SIDE
    spot_a = jnp.where(owner == row, 16 + local, dz * SIDE + dx)
    spot_b = jnp.where(owner == row, 16 + local, dx * SIDE + dz)
    first = pairs[:, 0] % blocks

    arrived = []
    for start, width in zip(starts, WIDTHS):
        send_a, send_b = pick(wants_z, wants_x, held_a, held_b, start // 2, width // 2)
        table_a = [send_a[0]] + [shift_z(send_a[d], d) for d in range(1, SIDE)] + [held_a[0]]
        table_b = [send_b[0]] + [shift_x(send_b[d], d) for d in range(1, SIDE)] + [held_b[0]]
        arrived.append((table_a, table_b))
    outs = []
    kept = None
    for (table_a, table_b), start, width in zip(arrived, starts, WIDTHS):
        slots, lists = grouped(first, spot_a, spot_b, TILE // width)
        if kept is not None:
            lists, kept_now = lax.optimization_barrier((lists, kept))
            outs[-1] = (kept_now,) + outs[-1][1:]
        mine, theirs = products(
            lists, slots, left_x, left_s, table_a, table_b, start // 2, width // 2, tiles
        )
        kept, *coded = merge(mine, swap_cores(theirs))
        moved = [shift_y(code, d + 1) for d, code in enumerate(coded)]
        outs.append((kept, moved, width // 64))
    return jnp.concatenate([finish(*out) for out in outs], axis=-1)


def solution(mesh):
    placed = (P("row", "col"), P("row", "col"), P("row", "col"), P("row", None))
    return jax.shard_map(
        shards, mesh=mesh, in_specs=placed, out_specs=P("row", "col", None), check_vma=False
    )
```

```python
import functools

import jax
import jax.numpy as jnp
from jax import lax
from jax.experimental import pallas as pl
from jax.experimental.pallas import tpu as pltpu
from jax.sharding import PartitionSpec as P


TILE = 256
SIDE = 4
WIDTHS = (64, 64)
LANES = 128
ROWS = 32
TOP = 32700.0
LENGTH = 16 * ROWS + 16

ANY = pl.BlockSpec(memory_space=pl.ANY)
SMEM = pl.BlockSpec(memory_space=pltpu.SMEM)
VMEM = pl.BlockSpec(memory_space=pltpu.VMEM)


def shift_x(value, step):
    perm = [(r, ((r // SIDE + step) % SIDE) * SIDE + r % SIDE) for r in range(SIDE * SIDE)]
    return lax.ppermute(value, "row", perm)


def shift_z(value, step):
    perm = [(r, (r // SIDE) * SIDE + (r % SIDE + step) % SIDE) for r in range(SIDE * SIDE)]
    return lax.ppermute(value, "row", perm)


def shift_y(value, step):
    perm = [(c, ((c // 2 + step) % SIDE) * 2 + c % 2) for c in range(SIDE * 2)]
    return lax.ppermute(value, "col", perm)


def swap_cores(value):
    return lax.ppermute(value, "col", [(c, c ^ 1) for c in range(SIDE * 2)])


def pick_kernel(offset, *refs):
    wants_z, wants_x = refs[0:4], refs[4:8]
    held = (refs[8:13], refs[13:18])
    outs = (refs[18:22], refs[22:26])
    sems = refs[26]
    part = pl.ds(offset, outs[0][0].shape[1])
    row = lax.axis_index("row")
    x, z = row // SIDE, row % SIDE
    waits = []
    for half in range(2):
        own, plus, minus, far_low, far_high = held[half]
        for away in range(SIDE):
            for near in range(SIDE):
                if away == 0 and near == 0:
                    continue
                if half == 0:
                    choice = wants_z[away][((x + SIDE - near) % SIDE) * SIDE + z]
                else:
                    choice = wants_x[away][x * SIDE + (z + SIDE - near) % SIDE]
                target = outs[half][away].at[near]
                sem = sems.at[half, away, near]
                if near == 2:
                    @pl.when(choice < 2)
                    def _():
                        pltpu.make_async_copy(far_low.at[choice, part], target, sem).start()

                    @pl.when(choice >= 2)
                    def _():
                        pltpu.make_async_copy(far_high.at[choice - 2, part], target, sem).start()
                else:
                    origin = {0: own, 1: plus, 3: minus}[near]
                    pltpu.make_async_copy(origin.at[choice, part], target, sem).start()
                waits.append(pltpu.make_async_copy(own.at[0, part], target, sem))
    for copy in waits:
        copy.wait()


def pick(wants_z, wants_x, held_a, held_b, offset, rows):
    piece = jax.ShapeDtypeStruct((SIDE, rows, held_a[0].shape[2]), held_a[0].dtype)
    outs = pl.pallas_call(
        functools.partial(pick_kernel, offset),
        out_shape=[piece] * 8,
        in_specs=[SMEM] * 8 + [ANY] * 10,
        out_specs=[VMEM] * 8,
        scratch_shapes=[pltpu.SemaphoreType.DMA((2, SIDE, SIDE))],
    )(*wants_z, *wants_x, *held_a, *held_b)
    return outs[:4], outs[4:]


def encode(value, out):
    count = value.shape[0]
    peak = jnp.maximum(jnp.max(jnp.abs(value), axis=1), 1e-30)
    level = jnp.ceil(jnp.log2(peak) * 256.0)
    factor = jnp.exp2(level * (-1.0 / 256.0)) * TOP
    code = jnp.round(value * factor[:, None, :]).astype(jnp.int32).astype(jnp.int16)
    out[pl.ds(0, count * ROWS)] = code.reshape(count * ROWS, LANES)
    out[pl.ds(count * ROWS, count)] = level.astype(jnp.int32).astype(jnp.int16)


def product_kernel(offset, rows, slots, *refs):
    group_first, group_start, slot_tile, slot_a, slot_b = refs[0:5]
    lefts = refs[5:9]
    tables = (refs[9:14], refs[14:19])
    kept, coded = refs[19], refs[20:23]
    left, held_a, held_b, acc, sems, left_sems, out_sem = refs[23:]
    y = lax.axis_index("col") // 2
    features = lefts[0].shape[2]
    width = 2 * rows
    group = TILE // width
    blocks = kept.shape[0]
    copies = []
    for half, held in enumerate((held_a, held_b)):
        for place in range(5):
            source = tables[half][place]
            if place == 4:
                source = source.at[:, pl.ds(offset, rows)]
            copies.append(
                pltpu.make_async_copy(source, held.at[pl.ds(place * SIDE, SIDE)], sems.at[half, place])
            )
    left_copies = []
    for block in range(SIDE):
        for n in range(4):
            target = left.at[block, pl.ds(n % 2 * TILE, TILE), pl.ds(n // 2 * features, features)]
            left_copies.append(pltpu.make_async_copy(lefts[n].at[block], target, left_sems.at[block, n]))
    for copy in copies + left_copies:
        copy.start()
    for copy in copies:
        copy.wait()

    def one(slot, carry):
        for block in range(SIDE):
            @pl.when(group_start[block] == slot)
            def _():
                for copy in left_copies[4 * block : 4 * block + 4]:
                    copy.wait()

        right = []
        for g in range(group):
            right += [held_a[slot_a[slot * group + g]], held_b[slot_b[slot * group + g]]]
        out = lax.dot_general(
            left[group_first[slot]],
            jnp.concatenate(right, axis=0),
            (((1,), (1,)), ((), ())),
            preferred_element_type=jnp.float32,
        )
        for g in range(group):
            tile = slot_tile[slot * group + g]
            cross_x = out[:TILE, g * width : (g + 1) * width]
            cross_s = out[TILE:, g * width : (g + 1) * width]
            parts = jnp.concatenate([cross_x, cross_s], axis=1).reshape(SIDE, 2, ROWS, LANES)
            for target in range(SIDE):
                away = (target + SIDE - y) % SIDE
                acc[away, pl.ds(tile * 2, 2)] = parts[target]
        return carry

    lax.fori_loop(0, slots, one, 0, unroll=3)
    for block in range(SIDE):
        @pl.when(group_start[block] >= slots)
        def _():
            for copy in left_copies[4 * block : 4 * block + 4]:
                copy.wait()

    keep = pltpu.make_async_copy(acc.at[0, pl.ds(0, blocks)], kept, out_sem)
    keep.start()
    for d in range(1, SIDE):
        for start in range(0, blocks, 16):
            encode(acc[d, pl.ds(start, 16)], coded[d - 1].at[pl.ds(start // 16 * LENGTH, LENGTH)])
    keep.wait()


def grouped(first, spot_a, spot_b, group):
    tiles = first.shape[0]
    slots = (tiles + (group - 1) * SIDE) // group
    kinds = jnp.arange(SIDE, dtype=jnp.int32)
    order = jnp.arange(tiles, dtype=jnp.int32)
    same = first[:, None] == first[None, :]
    rank = jnp.sum(jnp.where(same & (order[None, :] < order[:, None]), 1, 0), axis=1)
    counts = jnp.sum(jnp.where(first[None, :] == kinds[:, None], 1, 0), axis=1)
    sizes = (counts + group - 1) // group
    starts = jnp.sum(jnp.where(kinds[None, :] < kinds[:, None], sizes[None, :], 0), axis=1)
    start = jnp.sum(jnp.where(first[:, None] == kinds[None, :], starts[None, :], 0), axis=1)
    place = start * group + rank
    chosen = place[None, :] == jnp.arange(slots * group, dtype=jnp.int32)[:, None]
    used = jnp.any(chosen, axis=1)
    pull = lambda v: jnp.sum(jnp.where(chosen, v[None, :], 0), axis=1)
    slot_tile = jnp.where(used, pull(order), tiles)
    slot_a = jnp.where(used, pull(spot_a), 16)
    slot_b = jnp.where(used, pull(spot_b), 16)
    past = jnp.arange(slots, dtype=jnp.int32)[:, None] >= starts[None, :]
    group_first = jnp.sum(jnp.where(past, 1, 0), axis=1) - 1
    return slots, (group_first, starts, slot_tile, slot_a, slot_b)


def products(lists, slots, lefts, table_a, table_b, offset, rows, tiles):
    features = 2 * lefts[0].shape[2]
    blocks = 2 * tiles
    code = jax.ShapeDtypeStruct((blocks // 16 * LENGTH, LANES), jnp.int16)
    return pl.pallas_call(
        functools.partial(product_kernel, offset, rows, slots),
        out_shape=[jax.ShapeDtypeStruct((blocks, ROWS, LANES), jnp.float32)] + [code] * 3,
        in_specs=[SMEM] * 5 + [ANY] * 14,
        out_specs=[ANY] + [VMEM] * 3,
        scratch_shapes=[
            pltpu.VMEM((SIDE, 2 * TILE, features), jnp.bfloat16),
            pltpu.VMEM((20, rows, features), jnp.bfloat16),
            pltpu.VMEM((20, rows, features), jnp.bfloat16),
            pltpu.VMEM((SIDE, blocks + 2, ROWS, LANES), jnp.float32),
            pltpu.SemaphoreType.DMA((2, 5)),
            pltpu.SemaphoreType.DMA((SIDE, 4)),
            pltpu.SemaphoreType.DMA,
        ],
    )(*lists, *lefts, *table_a, *table_b)


def finish_kernel(kept, *refs):
    coded, mine, theirs = refs[:3], refs[3], refs[4]
    core = lax.axis_index("col") % 2
    count = kept.shape[0]
    total = kept[...]
    for ref in coded:
        code = ref[pl.ds(0, count * ROWS)].astype(jnp.int32).astype(jnp.float32)
        level = ref[pl.ds(count * ROWS, count)].astype(jnp.int32).astype(jnp.float32)
        factor = jnp.exp2(level * (1.0 / 256.0)) * (1.0 / TOP)
        total = total + code.reshape(count, ROWS, LANES) * factor[:, None, :]
    pairs = (total[..., : LANES // 2] * total[..., LANES // 2 :]).reshape(count // 2, 2, ROWS, LANES // 2)
    mine[...] = jnp.where(core == 0, pairs[:, 0], pairs[:, 1])
    theirs[...] = jnp.where(core == 0, pairs[:, 1], pairs[:, 0])


def finish(kept, coded):
    blocks = kept.shape[0]
    steps = blocks // 16
    out_block = pl.BlockSpec((8, ROWS, LANES // 2), lambda s: (s, 0, 0))
    return pl.pallas_call(
        finish_kernel,
        grid=(steps,),
        out_shape=[jax.ShapeDtypeStruct((8 * steps, ROWS, LANES // 2), jnp.float32)] * 2,
        in_specs=[pl.BlockSpec((16, ROWS, LANES), lambda s: (s, 0, 0))]
        + [pl.BlockSpec((LENGTH, LANES), lambda s: (s, 0))] * 3,
        out_specs=[out_block, out_block],
        name="finish",
    )(kept, *coded)


def gather_ring(own, shift):
    plus = shift(own, 1)
    minus = shift(own, SIDE - 1)
    far_low = shift(plus[:2], 1)
    far_high = shift(minus[2:], SIDE - 1)
    return own, plus, minus, far_low, far_high


def shards(primal_rows, dual_rows, weight_rows, pairs):
    row = lax.axis_index("row")
    x, z = row // SIDE, row % SIDE
    features = primal_rows.shape[1]
    blocks = primal_rows.shape[0] // TILE
    tiles = pairs.shape[0]
    core = lax.axis_index("col") % 2
    weight = weight_rows.reshape(blocks, TILE, features)
    columns = TILE // 2
    starts = [sum(WIDTHS[:k]) for k in range(len(WIDTHS))]
    given = lax.dynamic_slice_in_dim(weight, (1 - core) * columns, columns, 1)
    gotten = swap_cores(given)
    owned = lax.dynamic_slice_in_dim(weight, core * columns, columns, 1)
    owned = jnp.concatenate([owned, gotten], axis=2)
    half_a = [owned[:, s : s + w // 2] for s, w in zip(starts, WIDTHS)]
    half_b = [owned[:, s + w // 2 : s + w] for s, w in zip(starts, WIDTHS)]
    held_a = gather_ring(jnp.concatenate(half_a, axis=1), shift_x)
    held_b = gather_ring(jnp.concatenate(half_b, axis=1), shift_z)
    lefts = [primal_rows, dual_rows, swap_cores(primal_rows), swap_cores(dual_rows)]
    lefts = [v.reshape(blocks, TILE, features) for v in lefts]

    second = pairs[:, 1]
    owner, local = second // blocks, second % blocks
    hit = owner[:, None] == jnp.arange(SIDE * SIDE, dtype=jnp.int32)[None, :]
    want = jnp.max(jnp.where(hit, local[:, None], 0), axis=0)
    wants_z = [want] + [shift_z(want, SIDE - d) for d in range(1, SIDE)]
    wants_x = [want] + [shift_x(want, SIDE - d) for d in range(1, SIDE)]
    dx = (x + SIDE - owner // SIDE) % SIDE
    dz = (z + SIDE - owner % SIDE) % SIDE
    spot_a = jnp.where(owner == row, 16 + local, dz * SIDE + dx)
    spot_b = jnp.where(owner == row, 16 + local, dx * SIDE + dz)
    first = pairs[:, 0] % blocks

    arrived = []
    for start, width in zip(starts, WIDTHS):
        send_a, send_b = pick(wants_z, wants_x, held_a, held_b, start // 2, width // 2)
        table_a = [send_a[0]] + [shift_z(send_a[d], d) for d in range(1, SIDE)] + [held_a[0]]
        table_b = [send_b[0]] + [shift_x(send_b[d], d) for d in range(1, SIDE)] + [held_b[0]]
        arrived.append((table_a, table_b))
    outs = []
    for (table_a, table_b), start, width in zip(arrived, starts, WIDTHS):
        slots, lists = grouped(first, spot_a, spot_b, TILE // width)
        kept, *coded = products(
            lists, slots, lefts, table_a, table_b, start // 2, width // 2, tiles
        )
        moved = [shift_y(code, d + 1) for d, code in enumerate(coded)]
        mine, theirs = finish(kept, moved)
        outs.append((mine, swap_cores(theirs)))
    mine = jnp.concatenate([m for m, _ in outs], axis=-1)
    theirs = jnp.concatenate([t for _, t in outs], axis=-1)
    low = jnp.where(core == 0, mine, theirs)
    high = jnp.where(core == 0, theirs, mine)
    return jnp.concatenate([low, high], axis=-1)


def solution(mesh):
    placed = (P("row", "col"), P("row", "col"), P("row", "col"), P("row", None))
    return jax.shard_map(
        shards, mesh=mesh, in_specs=placed, out_specs=P("row", "col", None), check_vma=False
    )
```

```python
import functools

import jax
import jax.numpy as jnp
from jax import lax
from jax.experimental import pallas as pl
from jax.experimental.pallas import tpu as pltpu
from jax.sharding import PartitionSpec as P


TILE = 256
SIDE = 4
WIDTHS = (64, 64)
LANES = 128
ROWS = 32
TOP = 32700.0
LENGTH = 16 * ROWS + 16

ANY = pl.BlockSpec(memory_space=pl.ANY)
SMEM = pl.BlockSpec(memory_space=pltpu.SMEM)
VMEM = pl.BlockSpec(memory_space=pltpu.VMEM)
LEFT = pl.BlockSpec(memory_space=pltpu.VMEM)


def shift_x(value, step):
    perm = [(r, ((r // SIDE + step) % SIDE) * SIDE + r % SIDE) for r in range(SIDE * SIDE)]
    return lax.ppermute(value, "row", perm)


def shift_z(value, step):
    perm = [(r, (r // SIDE) * SIDE + (r % SIDE + step) % SIDE) for r in range(SIDE * SIDE)]
    return lax.ppermute(value, "row", perm)


def shift_y(value, step):
    perm = [(c, ((c // 2 + step) % SIDE) * 2 + c % 2) for c in range(SIDE * 2)]
    return lax.ppermute(value, "col", perm)


def swap_cores(value):
    return lax.ppermute(value, "col", [(c, c ^ 1) for c in range(SIDE * 2)])


def pick_kernel(offset, *refs):
    wants_z, wants_x = refs[0:4], refs[4:8]
    held = (refs[8:13], refs[13:18])
    outs = (refs[18:22], refs[22:26])
    sems = refs[26]
    part = pl.ds(offset, outs[0][0].shape[1])
    row = lax.axis_index("row")
    x, z = row // SIDE, row % SIDE
    waits = []
    for half in range(2):
        own, plus, minus, far_low, far_high = held[half]
        for away in range(SIDE):
            for near in range(SIDE):
                if away == 0 and near == 0:
                    continue
                if half == 0:
                    choice = wants_z[away][((x + SIDE - near) % SIDE) * SIDE + z]
                else:
                    choice = wants_x[away][x * SIDE + (z + SIDE - near) % SIDE]
                target = outs[half][away].at[near]
                sem = sems.at[half, away, near]
                if near == 2:
                    @pl.when(choice < 2)
                    def _():
                        pltpu.make_async_copy(far_low.at[choice, part], target, sem).start()

                    @pl.when(choice >= 2)
                    def _():
                        pltpu.make_async_copy(far_high.at[choice - 2, part], target, sem).start()
                else:
                    origin = {0: own, 1: plus, 3: minus}[near]
                    pltpu.make_async_copy(origin.at[choice, part], target, sem).start()
                waits.append(pltpu.make_async_copy(own.at[0, part], target, sem))
    for copy in waits:
        copy.wait()


def pick(wants_z, wants_x, held_a, held_b, offset, rows):
    piece = jax.ShapeDtypeStruct((SIDE, rows, held_a[0].shape[2]), held_a[0].dtype)
    outs = pl.pallas_call(
        functools.partial(pick_kernel, offset),
        out_shape=[piece] * 8,
        in_specs=[SMEM] * 8 + [ANY] * 10,
        out_specs=[VMEM] * 8,
        scratch_shapes=[pltpu.SemaphoreType.DMA((2, SIDE, SIDE))],
        compiler_params=pltpu.CompilerParams(vmem_limit_bytes=16 << 20),
    )(*wants_z, *wants_x, *held_a, *held_b)
    return outs[:4], outs[4:]


def encode(value, out):
    count = value.shape[0]
    peak = jnp.maximum(jnp.max(jnp.abs(value), axis=1), 1e-30)
    level = jnp.ceil(jnp.log2(peak) * 256.0)
    factor = jnp.exp2(level * (-1.0 / 256.0)) * TOP
    code = jnp.round(value * factor[:, None, :]).astype(jnp.int32).astype(jnp.int16)
    out[pl.ds(0, count * ROWS)] = code.reshape(count * ROWS, LANES)
    out[pl.ds(count * ROWS, count)] = level.astype(jnp.int32).astype(jnp.int16)


def product_kernel(offset, rows, slots, lists, left, *refs):
    tables = (refs[0:5], refs[5:10])
    kept, coded = refs[10], refs[11:14]
    held_a, held_b, acc, sems, out_sem = refs[14:]
    y = lax.axis_index("col") // 2
    width = 2 * rows
    group = TILE // width
    blocks = kept.shape[0]
    places = slots * group
    copies = []
    for half, held in enumerate((held_a, held_b)):
        for place in range(5):
            source = tables[half][place]
            if place == 4:
                source = source.at[:, pl.ds(offset, rows)]
            copies.append(
                pltpu.make_async_copy(source, held.at[pl.ds(place * SIDE, SIDE)], sems.at[half, place])
            )
    for copy in copies:
        copy.start()
    for copy in copies:
        copy.wait()

    def one(slot, carry):
        right = []
        for g in range(group):
            place = slots + slot * group + g
            right += [held_a[lists[place + places]], held_b[lists[place + 2 * places]]]
        out = lax.dot_general(
            left[lists[slot]],
            jnp.concatenate(right, axis=0),
            (((1,), (1,)), ((), ())),
            preferred_element_type=jnp.float32,
        )
        for g in range(group):
            tile = lists[slots + slot * group + g]
            cross_x = out[:TILE, g * width : (g + 1) * width]
            cross_s = out[TILE:, g * width : (g + 1) * width]
            parts = jnp.concatenate([cross_x, cross_s], axis=1).reshape(SIDE, 2, ROWS, LANES)
            for target in range(SIDE):
                away = (target + SIDE - y) % SIDE
                acc[away, pl.ds(tile * 2, 2)] = parts[target]
        return carry

    lax.fori_loop(0, slots, one, 0, unroll=3)
    keep = pltpu.make_async_copy(acc.at[0, pl.ds(0, blocks)], kept, out_sem)
    keep.start()
    for d in range(1, SIDE):
        for start in range(0, blocks, 16):
            encode(acc[d, pl.ds(start, 16)], coded[d - 1].at[pl.ds(start // 16 * LENGTH, LENGTH)])
    keep.wait()


def grouped(first, spot_a, spot_b, group):
    tiles = first.shape[0]
    slots = (tiles + (group - 1) * SIDE) // group
    kinds = jnp.arange(SIDE, dtype=jnp.int32)
    order = jnp.arange(tiles, dtype=jnp.int32)
    same = first[:, None] == first[None, :]
    rank = jnp.sum(jnp.where(same & (order[None, :] < order[:, None]), 1, 0), axis=1)
    counts = jnp.sum(jnp.where(first[None, :] == kinds[:, None], 1, 0), axis=1)
    sizes = (counts + group - 1) // group
    starts = jnp.sum(jnp.where(kinds[None, :] < kinds[:, None], sizes[None, :], 0), axis=1)
    start = jnp.sum(jnp.where(first[:, None] == kinds[None, :], starts[None, :], 0), axis=1)
    place = start * group + rank
    chosen = place[None, :] == jnp.arange(slots * group, dtype=jnp.int32)[:, None]
    used = jnp.any(chosen, axis=1)
    pull = lambda v: jnp.sum(jnp.where(chosen, v[None, :], 0), axis=1)
    slot_tile = jnp.where(used, pull(order), tiles)
    slot_a = jnp.where(used, pull(spot_a), 16)
    slot_b = jnp.where(used, pull(spot_b), 16)
    past = jnp.arange(slots, dtype=jnp.int32)[:, None] >= starts[None, :]
    group_first = jnp.sum(jnp.where(past, 1, 0), axis=1) - 1
    return slots, jnp.concatenate([group_first, slot_tile, slot_a, slot_b])


def products(lists, slots, left, table_a, table_b, offset, rows, tiles):
    features = left.shape[2]
    blocks = 2 * tiles
    code = jax.ShapeDtypeStruct((blocks // 16 * LENGTH, LANES), jnp.int16)
    return pl.pallas_call(
        functools.partial(product_kernel, offset, rows, slots),
        out_shape=[jax.ShapeDtypeStruct((blocks, ROWS, LANES), jnp.float32)] + [code] * 3,
        in_specs=[SMEM] + [LEFT] + [ANY] * 10,
        out_specs=[ANY] + [VMEM] * 3,
        scratch_shapes=[
            pltpu.VMEM((20, rows, features), jnp.bfloat16),
            pltpu.VMEM((20, rows, features), jnp.bfloat16),
            pltpu.VMEM((SIDE, blocks + 2, ROWS, LANES), jnp.float32),
            pltpu.SemaphoreType.DMA((2, 5)),
            pltpu.SemaphoreType.DMA,
        ],
        compiler_params=pltpu.CompilerParams(vmem_limit_bytes=28 << 20),
    )(lists, pltpu.with_memory_space_constraint(left, pltpu.VMEM), *table_a, *table_b)


def finish_kernel(before, kept, *refs):
    coded, earlier, mine, theirs = refs[:3], refs[3 : 3 + 2 * before], refs[-2], refs[-1]
    core = lax.axis_index("col") % 2
    count = kept.shape[0]
    total = kept[...]
    for ref in coded:
        code = ref[pl.ds(0, count * ROWS)].astype(jnp.int32).astype(jnp.float32)
        level = ref[pl.ds(count * ROWS, count)].astype(jnp.int32).astype(jnp.float32)
        factor = jnp.exp2(level * (1.0 / 256.0)) * (1.0 / TOP)
        total = total + code.reshape(count, ROWS, LANES) * factor[:, None, :]
    pairs = (total[..., : LANES // 2] * total[..., LANES // 2 :]).reshape(count // 2, 2, ROWS, LANES // 2)
    first = jnp.where(core == 0, pairs[:, 0], pairs[:, 1])
    second = jnp.where(core == 0, pairs[:, 1], pairs[:, 0])
    if before:
        first = jnp.concatenate([earlier[0][...], first], axis=-1)
        second = jnp.concatenate([earlier[1][...], second], axis=-1)
    mine[...] = first
    theirs[...] = second


def finish(kept, coded, earlier):
    blocks = kept.shape[0]
    steps = blocks // 16
    before = 1 if earlier else 0
    lanes = LANES // 2 * (1 + before)
    half_block = pl.BlockSpec((8, ROWS, LANES // 2), lambda s: (s, 0, 0))
    out_block = pl.BlockSpec((8, ROWS, lanes), lambda s: (s, 0, 0))
    return pl.pallas_call(
        functools.partial(finish_kernel, before),
        grid=(steps,),
        out_shape=[jax.ShapeDtypeStruct((8 * steps, ROWS, lanes), jnp.float32)] * 2,
        in_specs=[pl.BlockSpec((16, ROWS, LANES), lambda s: (s, 0, 0))]
        + [pl.BlockSpec((LENGTH, LANES), lambda s: (s, 0))] * 3
        + [half_block] * (2 * before),
        out_specs=[out_block, out_block],
        compiler_params=pltpu.CompilerParams(vmem_limit_bytes=16 << 20),
        name="finish",
    )(kept, *coded, *earlier)


def gather_ring(own, shift):
    plus = shift(own, 1)
    minus = shift(own, SIDE - 1)
    far_low = shift(plus[:2], 1)
    far_high = shift(minus[2:], SIDE - 1)
    return own, plus, minus, far_low, far_high


def shards(primal_rows, dual_rows, weight_rows, pairs):
    row = lax.axis_index("row")
    x, z = row // SIDE, row % SIDE
    features = primal_rows.shape[1]
    blocks = primal_rows.shape[0] // TILE
    tiles = pairs.shape[0]
    core = lax.axis_index("col") % 2
    weight = weight_rows.reshape(blocks, TILE, features)
    columns = TILE // 2
    starts = [sum(WIDTHS[:k]) for k in range(len(WIDTHS))]
    given = lax.dynamic_slice_in_dim(weight, (1 - core) * columns, columns, 1)
    gotten = swap_cores(given)
    owned = lax.dynamic_slice_in_dim(weight, core * columns, columns, 1)
    owned = jnp.concatenate([owned, gotten], axis=2)
    half_a = [owned[:, s : s + w // 2] for s, w in zip(starts, WIDTHS)]
    half_b = [owned[:, s + w // 2 : s + w] for s, w in zip(starts, WIDTHS)]
    held_a = gather_ring(jnp.concatenate(half_a, axis=1), shift_x)
    held_b = gather_ring(jnp.concatenate(half_b, axis=1), shift_z)
    own = [v.reshape(blocks, TILE, features) for v in (primal_rows, dual_rows)]
    other = [swap_cores(v) for v in (primal_rows, dual_rows)]
    other = [v.reshape(blocks, TILE, features) for v in other]
    left = jnp.concatenate([jnp.concatenate(own, axis=1), jnp.concatenate(other, axis=1)], axis=2)

    second = pairs[:, 1]
    owner, local = second // blocks, second % blocks
    hit = owner[:, None] == jnp.arange(SIDE * SIDE, dtype=jnp.int32)[None, :]
    want = jnp.max(jnp.where(hit, local[:, None], 0), axis=0)
    wants_z = [want] + [shift_z(want, SIDE - d) for d in range(1, SIDE)]
    wants_x = [want] + [shift_x(want, SIDE - d) for d in range(1, SIDE)]
    dx = (x + SIDE - owner // SIDE) % SIDE
    dz = (z + SIDE - owner % SIDE) % SIDE
    spot_a = jnp.where(owner == row, 16 + local, dz * SIDE + dx)
    spot_b = jnp.where(owner == row, 16 + local, dx * SIDE + dz)
    first = pairs[:, 0] % blocks

    arrived = []
    for start, width in zip(starts, WIDTHS):
        send_a, send_b = pick(wants_z, wants_x, held_a, held_b, start // 2, width // 2)
        table_a = [send_a[0]] + [shift_z(send_a[d], d) for d in range(1, SIDE)] + [held_a[0]]
        table_b = [send_b[0]] + [shift_x(send_b[d], d) for d in range(1, SIDE)] + [held_b[0]]
        arrived.append((table_a, table_b))
    outs = []
    for (table_a, table_b), start, width in zip(arrived, starts, WIDTHS):
        slots, lists = grouped(first, spot_a, spot_b, TILE // width)
        kept, *coded = products(lists, slots, left, table_a, table_b, start // 2, width // 2, tiles)
        moved = [shift_y(code, d + 1) for d, code in enumerate(coded)]
        outs = finish(kept, moved, outs)
    mine, theirs = outs
    theirs = swap_cores(theirs)
    low = jnp.where(core == 0, mine, theirs)
    high = jnp.where(core == 0, theirs, mine)
    return jnp.concatenate([low, high], axis=-1)


def solution(mesh):
    placed = (P("row", "col"), P("row", "col"), P("row", "col"), P("row", None))
    return jax.shard_map(
        shards, mesh=mesh, in_specs=placed, out_specs=P("row", "col", None), check_vma=False
    )
```

```python
import functools

import jax
import jax.numpy as jnp
from jax import lax
from jax.experimental import pallas as pl
from jax.experimental.pallas import tpu as pltpu
from jax.sharding import PartitionSpec as P


TILE = 256
SIDE = 4
WIDTHS = (64, 64)
LANES = 128
ROWS = 32
TOP = 32700.0
LENGTH = 16 * ROWS + 16

ANY = pl.BlockSpec(memory_space=pl.ANY)
SMEM = pl.BlockSpec(memory_space=pltpu.SMEM)
VMEM = pl.BlockSpec(memory_space=pltpu.VMEM)
LEFT = pl.BlockSpec(memory_space=pltpu.VMEM)


def shift_x(value, step):
    perm = [(r, ((r // SIDE + step) % SIDE) * SIDE + r % SIDE) for r in range(SIDE * SIDE)]
    return lax.ppermute(value, "row", perm)


def shift_z(value, step):
    perm = [(r, (r // SIDE) * SIDE + (r % SIDE + step) % SIDE) for r in range(SIDE * SIDE)]
    return lax.ppermute(value, "row", perm)


def shift_y(value, step):
    perm = [(c, ((c // 2 + step) % SIDE) * 2 + c % 2) for c in range(SIDE * 2)]
    return lax.ppermute(value, "col", perm)


def swap_cores(value):
    return lax.ppermute(value, "col", [(c, c ^ 1) for c in range(SIDE * 2)])


def pick_kernel(offset, wants, *refs):
    held = (refs[0:8], refs[8:16])
    outs = (refs[16:20], refs[20:24])
    sems = refs[24]
    part = pl.ds(offset, outs[0][0].shape[1])
    row = lax.axis_index("row")
    x, z = row // SIDE, row % SIDE
    owners = SIDE * SIDE
    waits = []
    for away in range(1, SIDE + 1):
        for half in range(2):
            for near in range(SIDE):
                far = away % SIDE
                if far == 0 and near == 0:
                    continue
                if half == 0:
                    spot = ((x + SIDE - near) % SIDE) * SIDE + z
                else:
                    spot = x * SIDE + (z + SIDE - near) % SIDE
                choice = wants[(far + (half * (SIDE - 1) if far else 0)) * owners + spot]
                low, high = held[half][2 * near : 2 * near + 2]
                target = outs[half][far].at[near]
                sem = sems.at[half, far, near]

                @pl.when(choice < 2)
                def _():
                    pltpu.make_async_copy(low.at[choice, part], target, sem).start()

                @pl.when(choice >= 2)
                def _():
                    pltpu.make_async_copy(high.at[choice - 2, part], target, sem).start()

                waits.append(pltpu.make_async_copy(low.at[0, part], target, sem))
    for copy in waits:
        copy.wait()


def pick(wants, held_a, held_b, offset, rows):
    piece = jax.ShapeDtypeStruct((SIDE, rows, held_a[0].shape[2]), held_a[0].dtype)
    outs = pl.pallas_call(
        functools.partial(pick_kernel, offset),
        out_shape=[piece] * 8,
        in_specs=[SMEM] + [ANY] * 16,
        out_specs=[ANY] * 8,
        scratch_shapes=[pltpu.SemaphoreType.DMA((2, SIDE, SIDE))],
        compiler_params=pltpu.CompilerParams(vmem_limit_bytes=16 << 20),
    )(wants, *held_a, *held_b)
    return outs[:4], outs[4:]


def encode(value, out):
    count = value.shape[0]
    peak = jnp.maximum(jnp.max(jnp.abs(value), axis=1), 1e-30)
    level = jnp.ceil(jnp.log2(peak) * 256.0)
    factor = jnp.exp2(level * (-1.0 / 256.0)) * TOP
    code = jnp.round(value * factor[:, None, :]).astype(jnp.int32).astype(jnp.int16)
    out[pl.ds(0, count * ROWS)] = code.reshape(count * ROWS, LANES)
    out[pl.ds(count * ROWS, count)] = level.astype(jnp.int32).astype(jnp.int16)


def product_kernel(offset, rows, slots, lists, left, *refs):
    tables = (refs[0:6], refs[6:12])
    kept, coded = refs[12], refs[13:16]
    held_a, held_b, acc, sems, out_sem = refs[16:]
    y = lax.axis_index("col") // 2
    width = 2 * rows
    group = TILE // width
    blocks = kept.shape[0]
    places = slots * group
    copies = []
    for half, held in enumerate((held_a, held_b)):
        for place in range(6):
            source = tables[half][place]
            if place < SIDE:
                target = held.at[pl.ds(place * SIDE, SIDE)]
            else:
                source = source.at[:, pl.ds(offset, rows)]
                target = held.at[pl.ds(8 + 2 * place, 2)]
            copies.append(pltpu.make_async_copy(source, target, sems.at[half, place]))
    for copy in copies:
        copy.start()
    for copy in copies:
        copy.wait()

    def one(slot, carry):
        right = []
        for g in range(group):
            place = slots + slot * group + g
            right += [held_a[lists[place + places]], held_b[lists[place + 2 * places]]]
        out = lax.dot_general(
            left[lists[slot]],
            jnp.concatenate(right, axis=0),
            (((1,), (1,)), ((), ())),
            preferred_element_type=jnp.float32,
        )
        for g in range(group):
            tile = lists[slots + slot * group + g]
            cross_x = out[:TILE, g * width : (g + 1) * width]
            cross_s = out[TILE:, g * width : (g + 1) * width]
            parts = jnp.concatenate([cross_x, cross_s], axis=1).reshape(SIDE, 2, ROWS, LANES)
            for target in range(SIDE):
                away = (target + SIDE - y) % SIDE
                acc[away, pl.ds(tile * 2, 2)] = parts[target]
        return carry

    lax.fori_loop(0, slots, one, 0, unroll=3)
    keep = pltpu.make_async_copy(acc.at[0, pl.ds(0, blocks)], kept, out_sem)
    keep.start()
    for d in range(1, SIDE):
        for start in range(0, blocks, 16):
            encode(acc[d, pl.ds(start, 16)], coded[d - 1].at[pl.ds(start // 16 * LENGTH, LENGTH)])
    keep.wait()


def grouped(first, spot_a, spot_b, group):
    tiles = first.shape[0]
    slots = (tiles + (group - 1) * SIDE) // group
    kinds = jnp.arange(SIDE, dtype=jnp.int32)
    order = jnp.arange(tiles, dtype=jnp.int32)
    same = first[:, None] == first[None, :]
    rank = jnp.sum(jnp.where(same & (order[None, :] < order[:, None]), 1, 0), axis=1)
    counts = jnp.sum(jnp.where(first[None, :] == kinds[:, None], 1, 0), axis=1)
    sizes = (counts + group - 1) // group
    starts = jnp.sum(jnp.where(kinds[None, :] < kinds[:, None], sizes[None, :], 0), axis=1)
    start = jnp.sum(jnp.where(first[:, None] == kinds[None, :], starts[None, :], 0), axis=1)
    place = start * group + rank
    chosen = place[None, :] == jnp.arange(slots * group, dtype=jnp.int32)[:, None]
    used = jnp.any(chosen, axis=1)
    pull = lambda v: jnp.sum(jnp.where(chosen, v[None, :], 0), axis=1)
    slot_tile = jnp.where(used, pull(order), tiles)
    slot_a = jnp.where(used, pull(spot_a), 16)
    slot_b = jnp.where(used, pull(spot_b), 16)
    past = jnp.arange(slots, dtype=jnp.int32)[:, None] >= starts[None, :]
    group_first = jnp.sum(jnp.where(past, 1, 0), axis=1) - 1
    return slots, jnp.concatenate([group_first, slot_tile, slot_a, slot_b])


def products(lists, slots, left, table_a, table_b, offset, rows, tiles):
    features = left.shape[2]
    blocks = 2 * tiles
    code = jax.ShapeDtypeStruct((blocks // 16 * LENGTH, LANES), jnp.int16)
    return pl.pallas_call(
        functools.partial(product_kernel, offset, rows, slots),
        out_shape=[jax.ShapeDtypeStruct((blocks, ROWS, LANES), jnp.float32)] + [code] * 3,
        in_specs=[SMEM] + [LEFT] + [ANY] * 12,
        out_specs=[ANY] + [VMEM] * 3,
        scratch_shapes=[
            pltpu.VMEM((20, rows, features), jnp.bfloat16),
            pltpu.VMEM((20, rows, features), jnp.bfloat16),
            pltpu.VMEM((SIDE, blocks + 2, ROWS, LANES), jnp.float32),
            pltpu.SemaphoreType.DMA((2, 6)),
            pltpu.SemaphoreType.DMA,
        ],
        compiler_params=pltpu.CompilerParams(vmem_limit_bytes=28 << 20),
    )(lists, pltpu.with_memory_space_constraint(left, pltpu.VMEM), *table_a, *table_b)


def finish_kernel(before, kept, *refs):
    coded, earlier, mine, theirs = refs[:3], refs[3 : 3 + 2 * before], refs[-2], refs[-1]
    core = lax.axis_index("col") % 2
    count = kept.shape[0]
    total = kept[...]
    for ref in coded:
        code = ref[pl.ds(0, count * ROWS)].astype(jnp.int32).astype(jnp.float32)
        level = ref[pl.ds(count * ROWS, count)].astype(jnp.int32).astype(jnp.float32)
        factor = jnp.exp2(level * (1.0 / 256.0)) * (1.0 / TOP)
        total = total + code.reshape(count, ROWS, LANES) * factor[:, None, :]
    pairs = (total[..., : LANES // 2] * total[..., LANES // 2 :]).reshape(count // 2, 2, ROWS, LANES // 2)
    first = jnp.where(core == 0, pairs[:, 0], pairs[:, 1])
    second = jnp.where(core == 0, pairs[:, 1], pairs[:, 0])
    if before:
        first = jnp.concatenate([earlier[0][...], first], axis=-1)
        second = jnp.concatenate([earlier[1][...], second], axis=-1)
    mine[...] = first
    theirs[...] = second


def finish(kept, coded, earlier):
    blocks = kept.shape[0]
    steps = blocks // 16
    before = 1 if earlier else 0
    lanes = LANES // 2 * (1 + before)
    half_block = pl.BlockSpec((8, ROWS, LANES // 2), lambda s: (s, 0, 0))
    out_block = pl.BlockSpec((8, ROWS, lanes), lambda s: (s, 0, 0))
    return pl.pallas_call(
        functools.partial(finish_kernel, before),
        grid=(steps,),
        out_shape=[jax.ShapeDtypeStruct((8 * steps, ROWS, lanes), jnp.float32)] * 2,
        in_specs=[pl.BlockSpec((16, ROWS, LANES), lambda s: (s, 0, 0))]
        + [pl.BlockSpec((LENGTH, LANES), lambda s: (s, 0))] * 3
        + [half_block] * (2 * before),
        out_specs=[out_block, out_block],
        compiler_params=pltpu.CompilerParams(vmem_limit_bytes=16 << 20),
        name="finish",
    )(kept, *coded, *earlier)


def gather_ring(low, high, shift):
    plus_low = shift(low, 1)
    minus_high = shift(high, SIDE - 1)
    plus_high = shift(high, 1)
    minus_low = shift(low, SIDE - 1)
    far_low = shift(plus_low, 1)
    far_high = shift(minus_high, SIDE - 1)
    return [low, high, plus_low, plus_high, far_low, far_high, minus_low, minus_high]


def shards(primal_rows, dual_rows, weight_rows, pairs):
    row = lax.axis_index("row")
    x, z = row // SIDE, row % SIDE
    features = primal_rows.shape[1]
    blocks = primal_rows.shape[0] // TILE
    tiles = pairs.shape[0]
    core = lax.axis_index("col") % 2
    weight = weight_rows.reshape(blocks, TILE, features)
    columns = TILE // 2
    starts = [sum(WIDTHS[:k]) for k in range(len(WIDTHS))]
    given = lax.dynamic_slice_in_dim(weight, (1 - core) * columns, columns, 1)
    gotten = swap_cores(given)
    owned = lax.dynamic_slice_in_dim(weight, core * columns, columns, 1)
    owned = jnp.concatenate([owned, gotten], axis=2)

    def part(side, chosen):
        rows = [(s + side * w // 2, s + (side + 1) * w // 2) for s, w in zip(starts, WIDTHS)]
        return jnp.concatenate([owned[chosen, lo:hi] for lo, hi in rows], axis=1)

    low, high = slice(0, 2), slice(2, 4)
    held_a = gather_ring(part(0, low), part(0, high), shift_x)
    held_b = gather_ring(part(1, low), part(1, high), shift_z)
    own = [v.reshape(blocks, TILE, features) for v in (primal_rows, dual_rows)]
    other = [swap_cores(v) for v in (primal_rows, dual_rows)]
    other = [v.reshape(blocks, TILE, features) for v in other]
    left = jnp.concatenate([jnp.concatenate(own, axis=1), jnp.concatenate(other, axis=1)], axis=2)

    second = pairs[:, 1]
    owner, local = second // blocks, second % blocks
    hit = owner[:, None] == jnp.arange(SIDE * SIDE, dtype=jnp.int32)[None, :]
    want = jnp.max(jnp.where(hit, local[:, None], 0), axis=0)
    asked = [shift_z(want, SIDE - d) for d in range(1, SIDE)]
    asked += [shift_x(want, SIDE - d) for d in range(1, SIDE)]
    wants = jnp.concatenate([want] + asked)
    dx = (x + SIDE - owner // SIDE) % SIDE
    dz = (z + SIDE - owner % SIDE) % SIDE
    spot_a = jnp.where(owner == row, 16 + local, dz * SIDE + dx)
    spot_b = jnp.where(owner == row, 16 + local, dx * SIDE + dz)
    first = pairs[:, 0] % blocks

    arrived = []
    for start, width in zip(starts, WIDTHS):
        send_a, send_b = pick(wants, held_a, held_b, start // 2, width // 2)
        table_a, table_b = [send_a[0]], [send_b[0]]
        for d in range(1, SIDE):
            table_a.append(shift_z(send_a[d], d))
            table_b.append(shift_x(send_b[d], d))
        table_a += held_a[:2]
        table_b += held_b[:2]
        arrived.append((table_a, table_b))
    outs = []
    for (table_a, table_b), start, width in zip(arrived, starts, WIDTHS):
        slots, lists = grouped(first, spot_a, spot_b, TILE // width)
        kept, *coded = products(lists, slots, left, table_a, table_b, start // 2, width // 2, tiles)
        moved = [shift_y(code, d + 1) for d, code in enumerate(coded)]
        outs = finish(kept, moved, outs)
    mine, theirs = outs
    theirs = swap_cores(theirs)
    low = jnp.where(core == 0, mine, theirs)
    high = jnp.where(core == 0, theirs, mine)
    return jnp.concatenate([low, high], axis=-1)


def solution(mesh):
    placed = (P("row", "col"), P("row", "col"), P("row", "col"), P("row", None))
    return jax.shard_map(
        shards, mesh=mesh, in_specs=placed, out_specs=P("row", "col", None), check_vma=False
    )
```

```python
import functools

import jax
import jax.numpy as jnp
from jax import lax
from jax.experimental import pallas as pl
from jax.experimental.pallas import tpu as pltpu
from jax.sharding import PartitionSpec as P


TILE = 256
SIDE = 4
WIDTHS = (64, 64)
LANES = 128
ROWS = 32
TOP = 32700.0
LENGTH = 16 * ROWS + 16

ANY = pl.BlockSpec(memory_space=pl.ANY)
SMEM = pl.BlockSpec(memory_space=pltpu.SMEM)
VMEM = pl.BlockSpec(memory_space=pltpu.VMEM)
LEFT = pl.BlockSpec(memory_space=pltpu.VMEM)


def shift_x(value, step):
    perm = [(r, ((r // SIDE + step) % SIDE) * SIDE + r % SIDE) for r in range(SIDE * SIDE)]
    return lax.ppermute(value, "row", perm)


def shift_z(value, step):
    perm = [(r, (r // SIDE) * SIDE + (r % SIDE + step) % SIDE) for r in range(SIDE * SIDE)]
    return lax.ppermute(value, "row", perm)


def shift_y(value, step):
    perm = [(c, ((c // 2 + step) % SIDE) * 2 + c % 2) for c in range(SIDE * 2)]
    return lax.ppermute(value, "col", perm)


def swap_cores(value):
    return lax.ppermute(value, "col", [(c, c ^ 1) for c in range(SIDE * 2)])


def pick_kernel(offset, wants, *refs):
    held = (refs[0:8], refs[8:16])
    outs = (refs[16:20], refs[20:24])
    sems = refs[24]
    part = pl.ds(offset, outs[0][0].shape[1])
    row = lax.axis_index("row")
    x, z = row // SIDE, row % SIDE
    owners = SIDE * SIDE
    waits = []
    for away in range(1, SIDE + 1):
        for half in range(2):
            for near in range(SIDE):
                far = away % SIDE
                if far == 0 and near == 0:
                    continue
                if half == 0:
                    spot = ((x + SIDE - near) % SIDE) * SIDE + z
                else:
                    spot = x * SIDE + (z + SIDE - near) % SIDE
                choice = wants[(far + (half * (SIDE - 1) if far else 0)) * owners + spot]
                low, high = held[half][2 * near : 2 * near + 2]
                target = outs[half][far].at[near]
                sem = sems.at[half, far, near]

                @pl.when(choice < 2)
                def _():
                    pltpu.make_async_copy(low.at[choice, part], target, sem).start()

                @pl.when(choice >= 2)
                def _():
                    pltpu.make_async_copy(high.at[choice - 2, part], target, sem).start()

                waits.append(pltpu.make_async_copy(low.at[0, part], target, sem))
    for copy in waits:
        copy.wait()


def pick(wants, held_a, held_b, offset, rows):
    piece = jax.ShapeDtypeStruct((SIDE, rows, held_a[0].shape[2]), held_a[0].dtype)
    outs = pl.pallas_call(
        functools.partial(pick_kernel, offset),
        out_shape=[piece] * 8,
        in_specs=[SMEM] + [ANY] * 16,
        out_specs=[ANY] * 8,
        scratch_shapes=[pltpu.SemaphoreType.DMA((2, SIDE, SIDE))],
        compiler_params=pltpu.CompilerParams(vmem_limit_bytes=16 << 20),
    )(wants, *held_a, *held_b)
    return outs[:4], outs[4:]


def encode(value, out):
    count = value.shape[0]
    peak = jnp.maximum(jnp.max(jnp.abs(value), axis=1), 1e-30)
    level = jnp.ceil(jnp.log2(peak) * 256.0)
    factor = jnp.exp2(level * (-1.0 / 256.0)) * TOP
    code = jnp.round(value * factor[:, None, :]).astype(jnp.int32).astype(jnp.int16)
    out[pl.ds(0, count * ROWS)] = code.reshape(count * ROWS, LANES)
    out[pl.ds(count * ROWS, count)] = level.astype(jnp.int32).astype(jnp.int16)


def product_kernel(offset, rows, slots, lists, left, *refs):
    tables = (refs[0:6], refs[6:12])
    kept, coded = refs[12], refs[13:16]
    held_a, held_b, acc, sems, out_sem = refs[16:]
    y = lax.axis_index("col") // 2
    width = 2 * rows
    group = TILE // width
    blocks = kept.shape[0]
    places = slots * group
    copies = []
    for half, held in enumerate((held_a, held_b)):
        for place in range(6):
            source = tables[half][place]
            if place < SIDE:
                target = held.at[pl.ds(place * SIDE, SIDE)]
            else:
                source = source.at[:, pl.ds(offset, rows)]
                target = held.at[pl.ds(8 + 2 * place, 2)]
            copies.append(pltpu.make_async_copy(source, target, sems.at[half, place]))
    for copy in copies:
        copy.start()
    for copy in copies:
        copy.wait()

    def one(slot, carry):
        right = []
        for g in range(group):
            place = slots + slot * group + g
            right += [held_a[lists[place + places]], held_b[lists[place + 2 * places]]]
        out = lax.dot_general(
            left[lists[slot]],
            jnp.concatenate(right, axis=0),
            (((1,), (1,)), ((), ())),
            preferred_element_type=jnp.float32,
        )
        for g in range(group):
            tile = lists[slots + slot * group + g]
            cross_x = out[:TILE, g * width : (g + 1) * width]
            cross_s = out[TILE:, g * width : (g + 1) * width]
            parts = jnp.concatenate([cross_x, cross_s], axis=1).reshape(SIDE, 2, ROWS, LANES)
            for target in range(SIDE):
                away = (target + SIDE - y) % SIDE
                acc[away, pl.ds(tile * 2, 2)] = parts[target]
        return carry

    lax.fori_loop(0, slots, one, 0, unroll=9)
    keep = pltpu.make_async_copy(acc.at[0, pl.ds(0, blocks)], kept, out_sem)
    keep.start()
    for d in range(1, SIDE):
        for start in range(0, blocks, 16):
            encode(acc[d, pl.ds(start, 16)], coded[d - 1].at[pl.ds(start // 16 * LENGTH, LENGTH)])
    keep.wait()


def grouped(first, spot_a, spot_b, group):
    tiles = first.shape[0]
    slots = (tiles + (group - 1) * SIDE) // group
    kinds = jnp.arange(SIDE, dtype=jnp.int32)
    order = jnp.arange(tiles, dtype=jnp.int32)
    same = first[:, None] == first[None, :]
    rank = jnp.sum(jnp.where(same & (order[None, :] < order[:, None]), 1, 0), axis=1)
    counts = jnp.sum(jnp.where(first[None, :] == kinds[:, None], 1, 0), axis=1)
    sizes = (counts + group - 1) // group
    starts = jnp.sum(jnp.where(kinds[None, :] < kinds[:, None], sizes[None, :], 0), axis=1)
    start = jnp.sum(jnp.where(first[:, None] == kinds[None, :], starts[None, :], 0), axis=1)
    place = start * group + rank
    chosen = place[None, :] == jnp.arange(slots * group, dtype=jnp.int32)[:, None]
    used = jnp.any(chosen, axis=1)
    pull = lambda v: jnp.sum(jnp.where(chosen, v[None, :], 0), axis=1)
    slot_tile = jnp.where(used, pull(order), tiles)
    slot_a = jnp.where(used, pull(spot_a), 16)
    slot_b = jnp.where(used, pull(spot_b), 16)
    past = jnp.arange(slots, dtype=jnp.int32)[:, None] >= starts[None, :]
    group_first = jnp.sum(jnp.where(past, 1, 0), axis=1) - 1
    return slots, jnp.concatenate([group_first, slot_tile, slot_a, slot_b])


def products(lists, slots, left, table_a, table_b, offset, rows, tiles):
    features = left.shape[2]
    blocks = 2 * tiles
    code = jax.ShapeDtypeStruct((blocks // 16 * LENGTH, LANES), jnp.int16)
    return pl.pallas_call(
        functools.partial(product_kernel, offset, rows, slots),
        out_shape=[jax.ShapeDtypeStruct((blocks, ROWS, LANES), jnp.float32)] + [code] * 3,
        in_specs=[SMEM] + [LEFT] + [ANY] * 12,
        out_specs=[ANY] + [VMEM] * 3,
        scratch_shapes=[
            pltpu.VMEM((20, rows, features), jnp.bfloat16),
            pltpu.VMEM((20, rows, features), jnp.bfloat16),
            pltpu.VMEM((SIDE, blocks + 2, ROWS, LANES), jnp.float32),
            pltpu.SemaphoreType.DMA((2, 6)),
            pltpu.SemaphoreType.DMA,
        ],
        compiler_params=pltpu.CompilerParams(vmem_limit_bytes=28 << 20),
    )(lists, pltpu.with_memory_space_constraint(left, pltpu.VMEM), *table_a, *table_b)


def finish_kernel(before, kept, *refs):
    coded, earlier, mine, theirs = refs[:3], refs[3 : 3 + 2 * before], refs[-2], refs[-1]
    core = lax.axis_index("col") % 2
    count = kept.shape[0]
    total = kept[...]
    for ref in coded:
        code = ref[pl.ds(0, count * ROWS)].astype(jnp.int32).astype(jnp.float32)
        level = ref[pl.ds(count * ROWS, count)].astype(jnp.int32).astype(jnp.float32)
        factor = jnp.exp2(level * (1.0 / 256.0)) * (1.0 / TOP)
        total = total + code.reshape(count, ROWS, LANES) * factor[:, None, :]
    pairs = (total[..., : LANES // 2] * total[..., LANES // 2 :]).reshape(count // 2, 2, ROWS, LANES // 2)
    first = jnp.where(core == 0, pairs[:, 0], pairs[:, 1])
    second = jnp.where(core == 0, pairs[:, 1], pairs[:, 0])
    if before:
        first = jnp.concatenate([earlier[0][...], first], axis=-1)
        second = jnp.concatenate([earlier[1][...], second], axis=-1)
    mine[...] = first
    theirs[...] = second


def finish(kept, coded, earlier):
    blocks = kept.shape[0]
    steps = blocks // 16
    before = 1 if earlier else 0
    lanes = LANES // 2 * (1 + before)
    half_block = pl.BlockSpec((8, ROWS, LANES // 2), lambda s: (s, 0, 0))
    out_block = pl.BlockSpec((8, ROWS, lanes), lambda s: (s, 0, 0))
    return pl.pallas_call(
        functools.partial(finish_kernel, before),
        grid=(steps,),
        out_shape=[jax.ShapeDtypeStruct((8 * steps, ROWS, lanes), jnp.float32)] * 2,
        in_specs=[pl.BlockSpec((16, ROWS, LANES), lambda s: (s, 0, 0))]
        + [pl.BlockSpec((LENGTH, LANES), lambda s: (s, 0))] * 3
        + [half_block] * (2 * before),
        out_specs=[out_block, out_block],
        compiler_params=pltpu.CompilerParams(vmem_limit_bytes=16 << 20),
        name="finish",
    )(kept, *coded, *earlier)


def gather_ring(low, high, shift):
    plus_low = shift(low, 1)
    minus_high = shift(high, SIDE - 1)
    plus_high = shift(high, 1)
    minus_low = shift(low, SIDE - 1)
    far_low = shift(plus_low, 1)
    far_high = shift(minus_high, SIDE - 1)
    return [low, high, plus_low, plus_high, far_low, far_high, minus_low, minus_high]


def shards(primal_rows, dual_rows, weight_rows, pairs):
    row = lax.axis_index("row")
    x, z = row // SIDE, row % SIDE
    features = primal_rows.shape[1]
    blocks = primal_rows.shape[0] // TILE
    tiles = pairs.shape[0]
    core = lax.axis_index("col") % 2
    weight = weight_rows.reshape(blocks, TILE, features)
    columns = TILE // 2
    starts = [sum(WIDTHS[:k]) for k in range(len(WIDTHS))]
    given = lax.dynamic_slice_in_dim(weight, (1 - core) * columns, columns, 1)
    gotten = swap_cores(given)
    owned = lax.dynamic_slice_in_dim(weight, core * columns, columns, 1)
    owned = jnp.concatenate([owned, gotten], axis=2)

    def part(side, chosen):
        rows = [(s + side * w // 2, s + (side + 1) * w // 2) for s, w in zip(starts, WIDTHS)]
        return jnp.concatenate([owned[chosen, lo:hi] for lo, hi in rows], axis=1)

    low, high = slice(0, 2), slice(2, 4)
    held_a = gather_ring(part(0, low), part(0, high), shift_x)
    held_b = gather_ring(part(1, low), part(1, high), shift_z)
    own = [v.reshape(blocks, TILE, features) for v in (primal_rows, dual_rows)]
    other = [swap_cores(v) for v in (primal_rows, dual_rows)]
    other = [v.reshape(blocks, TILE, features) for v in other]
    left = jnp.concatenate([jnp.concatenate(own, axis=1), jnp.concatenate(other, axis=1)], axis=2)

    second = pairs[:, 1]
    owner, local = second // blocks, second % blocks
    hit = owner[:, None] == jnp.arange(SIDE * SIDE, dtype=jnp.int32)[None, :]
    want = jnp.max(jnp.where(hit, local[:, None], 0), axis=0)
    asked = [shift_z(want, SIDE - d) for d in range(1, SIDE)]
    asked += [shift_x(want, SIDE - d) for d in range(1, SIDE)]
    wants = jnp.concatenate([want] + asked)
    dx = (x + SIDE - owner // SIDE) % SIDE
    dz = (z + SIDE - owner % SIDE) % SIDE
    spot_a = jnp.where(owner == row, 16 + local, dz * SIDE + dx)
    spot_b = jnp.where(owner == row, 16 + local, dx * SIDE + dz)
    first = pairs[:, 0] % blocks

    arrived = []
    for start, width in zip(starts, WIDTHS):
        send_a, send_b = pick(wants, held_a, held_b, start // 2, width // 2)
        table_a, table_b = [send_a[0]], [send_b[0]]
        for d in range(1, SIDE):
            table_a.append(shift_z(send_a[d], d))
            table_b.append(shift_x(send_b[d], d))
        table_a += held_a[:2]
        table_b += held_b[:2]
        arrived.append((table_a, table_b))
    outs = []
    for (table_a, table_b), start, width in zip(arrived, starts, WIDTHS):
        slots, lists = grouped(first, spot_a, spot_b, TILE // width)
        kept, *coded = products(lists, slots, left, table_a, table_b, start // 2, width // 2, tiles)
        moved = []
        for d, code in enumerate(coded):
            moved.append(shift_y(code, d + 1))
        outs = finish(kept, moved, outs)
    mine, theirs = outs
    theirs = swap_cores(theirs)
    low = jnp.where(core == 0, mine, theirs)
    high = jnp.where(core == 0, theirs, mine)
    return jnp.concatenate([low, high], axis=-1)


def solution(mesh):
    placed = (P("row", "col"), P("row", "col"), P("row", "col"), P("row", None))
    return jax.shard_map(
        shards, mesh=mesh, in_specs=placed, out_specs=P("row", "col", None), check_vma=False
    )
```
